512 devices in a mesh: sec: 16 (over z_hi, x), row: 32 (over y, z_lo, core).
Axes of the slice: x: 4, y: 8, z: 8 (z_hi: 4, z_lo: 2; z = z_hi * 2 + z_lo), core: 2. Of those that a mesh axis runs over, the one named last changes fastest.
Arguments:
- source: bfloat16 [16, 8192, 2048], P('sec', 'row'), may hold values from -120 to 120, as said below
- routes: int32 [16, 1024], P('sec', 'row'), may hold values from 0 to 1023, as said below
- offsets: float32 [16, 2, 1024], P('sec', None, 'row'), may hold values from 0 to 1
Outputs:
- rendered: float32 [16, 8192, 2048], P('sec', 'row')
- flows: float32 [16, 2, 128, 32], P('sec', None, 'row')
The draws below stay inside these ranges and needn't reach their ends.
Inputs may be any that keep to these rules, and one draw needn't show every extreme that they name: `source`: magnitudes vary from row to row and column to column. `routes`: the 32 output blocks of one device's strip read at most 2 source blocks from the strip of any one device of the same section, and exactly 2 from some device.
All inputs are finite; a program needn't handle non-finite values.
Results may differ from the reference program's by a relative error of at most 0.0003.
Values may be sent and summed in bfloat16 or wider, within the bound.
No kernel may reach another device: no remote copies, remote signals or barrier semaphores. Data moves between devices by JAX's collectives and lax.ppermute only.
A program may use at most 64 MiB of HBM per device.

```python
import jax
import jax.numpy as jnp
from jax import lax

IMG_W = 2048
SECTIONS = 16
H = 8192
GB = 32
BLOCKS = 1024
CAP = 2
N_ROW = 32


def draw_source(key, part):
    subkeys = jax.random.split(key, 4)
    common = jnp.clip(jax.random.normal(subkeys[0], (1, H, IMG_W), jnp.float32), -3.0, 3.0)
    own = jnp.clip(jax.random.normal(subkeys[3], (SECTIONS, H, IMG_W), jnp.float32), -3.0, 3.0)
    baseline = common + 0.3 * own
    row_scale = jnp.exp(jax.random.uniform(subkeys[1], (1, H, 1), jnp.float32) * jnp.log(10.0))
    col_scale = jnp.exp(jax.random.uniform(subkeys[2], (1, 1, IMG_W), jnp.float32) * jnp.log(3.0))
    return (baseline * row_scale * col_scale).astype(jnp.bfloat16)


def draw_routes(key, part):

    def one_strip(strip_key, strip_number):
        subkeys = jax.random.split(strip_key, 4)
        drawn_device = jax.random.randint(subkeys[0], (), 0, N_ROW)
        full_device = jnp.where(strip_number == 0, N_ROW // 2, drawn_device).astype(jnp.int32)
        others = (full_device + 1 + jnp.arange((N_ROW - 1) * CAP) // CAP) % N_ROW
        shuffled = jax.random.permutation(subkeys[1], others)
        devices = jnp.concatenate([jnp.full((CAP,), full_device, dtype=jnp.int32), shuffled[:GB - CAP].astype(jnp.int32)])
        devices = jax.random.permutation(subkeys[2], devices)
        within = jax.random.randint(subkeys[3], (GB,), 0, GB)
        return (devices * GB + within).astype(jnp.int32)
    strip_keys = jax.random.split(jax.random.fold_in(key, 7), SECTIONS * N_ROW)
    numbers = (jnp.arange(SECTIONS * N_ROW, dtype=jnp.int32) % N_ROW).astype(jnp.int32)
    every = jax.vmap(one_strip)(strip_keys, numbers)
    return every.reshape(SECTIONS, BLOCKS).astype(jnp.int32)


def shard_levels(rng, shape, shards, low, high):
    loudness, own = 1.0, jax.random.fold_in(rng, 6)
    for dim, shards_of in shards:
        heights = jnp.exp(jax.random.uniform(jax.random.fold_in(own, dim), (shards_of,), jnp.float32, low / len(shards), high / len(shards)))
        loudness = loudness * jnp.repeat(heights, shape[dim] // shards_of).reshape([-1 if axis == dim else 1 for axis in range(len(shape))])
    return loudness


def setup_inputs(seed: int = 0) -> dict:
    key_list = jax.random.split(jax.random.key(seed), 4)
    source = draw_source(jax.random.fold_in(key_list[3], 71), 0)
    routes = draw_routes(jax.random.fold_in(key_list[3], 71), 0)
    offsets = jnp.clip(1.0 * jax.random.uniform(key_list[2], (SECTIONS, 2, BLOCKS), jnp.float32) ** shard_levels(key_list[2], (SECTIONS, 2, BLOCKS), ((0, 16), (2, 32)), -0.2, 0.2), 0.0, 1.0)
    return dict(source=source, routes=routes, offsets=offsets)


peak_floor = 64.0
tiny_value = 1e-06

def bilinear(square, downward, across):
    step_right = jnp.concatenate([square[:, :, 1:], square[:, :, -1:]], 2)
    step_down = jnp.concatenate([square[:, 1:], square[:, -1:]], 1)
    step_both = jnp.concatenate([step_right[:, 1:], step_right[:, -1:]], 1)
    downward = downward[:, None, None]
    across = across[:, None, None]
    upper_row = (1.0 - across) * square + across * step_right
    lower_row = (1.0 - across) * step_down + across * step_both
    return (1.0 - downward) * upper_row + downward * lower_row

def render_section(section, route, fractions):
    height, width = section.shape
    block_rows = height // 128
    block_cols = width // 128
    tiles = section.reshape(block_rows, 128, block_cols, 128).transpose(0, 2, 1, 3).reshape(-1, 128, 128)
    picked = tiles[route].astype(jnp.float32)
    made = bilinear(picked, fractions[0], fractions[1])
    return made.reshape(block_rows, block_cols, 128, 128).transpose(0, 2, 1, 3).reshape(height, width)

def patches_of(image):
    height, width = image.shape
    padded = jnp.pad(image.astype(jnp.float32), ((32, 0), (32, 0)))[:height, :width]
    tiles = padded.reshape(height // 64, 64, width // 64, 64).transpose(0, 2, 1, 3)
    centred = tiles - lax.optimization_barrier(jnp.mean(tiles, axis=(2, 3), keepdims=True))
    return centred / jnp.sqrt(lax.optimization_barrier(jnp.mean(centred * centred, axis=(2, 3), keepdims=True)) + tiny_value)

def parabola(nearby):
    profile_down = (nearby[..., 0] + 2.0 * nearby[..., 1] + nearby[..., 2]) * 0.25
    profile_across = (nearby[..., 0, :] + 2.0 * nearby[..., 1, :] + nearby[..., 2, :]) * 0.25
    curve_down = jnp.maximum(2.0 * profile_down[..., 1] - profile_down[..., 0] - profile_down[..., 2], peak_floor)
    curve_across = jnp.maximum(2.0 * profile_across[..., 1] - profile_across[..., 0] - profile_across[..., 2], peak_floor)
    flow_down = (profile_down[..., 2] - profile_down[..., 0]) / (2.0 * curve_down)
    flow_across = (profile_across[..., 2] - profile_across[..., 0]) / (2.0 * curve_across)
    return jnp.stack([flow_down, flow_across], 0)

def pair_flow(first, second):
    spectrum_first = jnp.fft.fft2(patches_of(first))
    spectrum_second = jnp.fft.fft2(patches_of(second))
    correlation = jnp.fft.ifft2(jnp.conj(spectrum_first) * spectrum_second).real
    corner = jnp.array([63, 0, 1], dtype=jnp.int32)
    nearby = correlation[:, :, corner][:, :, :, corner]
    return parabola(nearby)

def reference(source, routes, offsets):
    rendered = lax.map(lambda packed: render_section(packed[0], packed[1], packed[2]), (source, routes, offsets))
    flows = lax.map(lambda packed: pair_flow(packed[0], packed[1]), (rendered[:-1], rendered[1:]))
    flows = jnp.concatenate([flows, jnp.zeros_like(flows[:1])], 0)
    return (rendered, flows)
```

```python
import functools

import jax
import jax.numpy as jnp
from jax import lax
from jax.experimental import pallas as pl
from jax.experimental.pallas import tpu as pltpu
from jax.sharding import PartitionSpec as P


peak_floor = 64.0
tiny_value = 1e-06
BLOCK = 128
PATCH = 64
SPLIT = 32
VMEM = pltpu.VMEM
SMEM = pltpu.SMEM
F32 = jnp.float32
BF16 = jnp.bfloat16


def spec(space):
    return pl.BlockSpec(memory_space=space)


def shape(dims, dtype):
    return jax.ShapeDtypeStruct(dims, dtype)


def params(limit=14 << 20):
    return pltpu.CompilerParams(vmem_limit_bytes=limit)


def cut_blocks(strip_ref, out_ref):
    wide = strip_ref.shape[1] // BLOCK
    for i in range(strip_ref.shape[0] // BLOCK):
        for k in range(wide):
            out_ref[i * wide + k] = strip_ref[i * BLOCK : (i + 1) * BLOCK, k * BLOCK : (k + 1) * BLOCK]


def blocks_of(strip):
    rows, cols = strip.shape
    return pl.pallas_call(
        cut_blocks,
        out_shape=shape((rows // BLOCK * (cols // BLOCK), BLOCK, BLOCK), strip.dtype),
        in_specs=[spec(VMEM)],
        out_specs=spec(VMEM),
        compiler_params=params(),
        cost_estimate=pl.CostEstimate(flops=0, bytes_accessed=2_000_000, transcendentals=0),
    )(strip)


def pack_requested(row_from, rows, picked_ref, blocks_ref, out_ref, sem):
    def one(i, carry):
        spot = picked_ref[i // 2, 0, i % 2]
        pltpu.make_async_copy(blocks_ref.at[spot, pl.ds(row_from, rows), :], out_ref.at[i], sem).start()
        return carry

    lax.fori_loop(0, out_ref.shape[0], one, 0, unroll=8)
    pltpu.make_async_copy(out_ref, out_ref, sem).wait()


def requested(picked, blocks, row_from, rows):
    slots = 2 * picked.shape[0]
    return pl.pallas_call(
        functools.partial(pack_requested, row_from, rows),
        out_shape=shape((slots, rows, BLOCK), blocks.dtype),
        in_specs=[spec(SMEM), spec(VMEM)],
        out_specs=spec(pl.ANY),
        scratch_shapes=[pltpu.SemaphoreType.DMA],
        compiler_params=params(55_000_000),
    )(picked, blocks)


def pack_for_sections(slot_ref, deep_ref, middle_ref, top_ref, bottom_ref, first_ref, next_ref):
    half = bottom_ref.shape[0]

    def one(b, carry):
        s = slot_ref[b]
        middle_ref[b] = deep_ref[s, pl.ds(0, 64), :]
        first_ref[pl.ds(b, 1), :] = deep_ref[s, pl.ds(0, 16), :].astype(F32)[0:1]
        next_ref[pl.ds(b, 1), :] = deep_ref[s, pl.ds(64, 16), :].astype(F32)[0:1]
        return carry

    lax.fori_loop(0, 2 * half, one, 0, unroll=4)

    def tails(b, carry):
        top_ref[b] = deep_ref[slot_ref[b], pl.ds(64, 32), :]
        bottom_ref[b] = deep_ref[slot_ref[half + b], pl.ds(64, 32), :]
        return carry

    lax.fori_loop(0, half, tails, 0, unroll=4)
    middle_ref[2 * half, pl.ds(0, 32), :] = next_ref[...].astype(BF16)
    middle_ref[2 * half, pl.ds(32, 32), :] = jnp.zeros((32, BLOCK), BF16)
    top_ref[half] = first_ref[...].astype(BF16)


def section_parts(slot, deep):
    count = slot.shape[0]
    half = count // 2
    return pl.pallas_call(
        pack_for_sections,
        out_shape=(
            shape((count + 1, 64, BLOCK), BF16),
            shape((half + 1, 32, BLOCK), BF16),
            shape((half, 32, BLOCK), BF16),
        ),
        in_specs=[spec(SMEM), spec(VMEM)],
        out_specs=(spec(VMEM), spec(VMEM), spec(VMEM)),
        scratch_shapes=[VMEM((count, BLOCK), F32), VMEM((count, BLOCK), F32)],
        compiler_params=params(),
    )(slot, deep)


def pack_shallow(slot_ref, shallow_ref, out_ref):
    def one(b, carry):
        out_ref[b] = shallow_ref[slot_ref[b]]
        return carry

    lax.fori_loop(0, out_ref.shape[0], one, 0, unroll=4)


def shallow_part(slot, shallow):
    return pl.pallas_call(
        pack_shallow,
        out_shape=shape((slot.shape[0], *shallow.shape[1:]), BF16),
        in_specs=[spec(SMEM), spec(VMEM)],
        out_specs=spec(VMEM),
        compiler_params=params(),
    )(slot, shallow)


def mixed_across(square, across):
    lane = lax.broadcasted_iota(jnp.int32, square.shape, 1)
    moved = jnp.where(lane == BLOCK - 1, square, pltpu.roll(square, BLOCK - 1, 1))
    return (1.0 - across) * square + across * moved


def render_rows(square, following, downward, across):
    rows = square.shape[0]
    mixed = mixed_across(square, across)
    below = mixed if following is None else mixed_across(following, across)
    row = lax.broadcasted_iota(jnp.int32, square.shape, 0)
    moved = jnp.where(row == rows - 1, below, pltpu.roll(mixed, rows - 1, 0))
    return (1.0 - downward) * mixed + downward * moved


def joined(made, carried):
    lane = lax.broadcasted_iota(jnp.int32, made.shape, 1)
    return jnp.where(lane < BLOCK - PATCH // 2, made, carried)


def same_patch():
    half = PATCH // 2
    one = lax.broadcasted_iota(jnp.int32, (BLOCK, BLOCK), 0)
    two = lax.broadcasted_iota(jnp.int32, (BLOCK, BLOCK), 1)
    return ((((one + half) // PATCH) % 2) == (((two + half) // PATCH) % 2)).astype(F32)


def per_patch(values):
    return jnp.dot(values, same_patch(), precision=lax.Precision.HIGHEST)


def filter_tiles(tall_ref, sums_ref, soft_ref, step_ref, bend_ref, power_ref):
    half = PATCH // 2
    sums_ref[...] = per_patch(sums_ref[...]) / float(PATCH * PATCH)

    def filtered(t, carry):
        b = tall_ref[t] - sums_ref[pl.ds(t, 1), :]
        lane = lax.broadcasted_iota(jnp.int32, b.shape, 1) % PATCH
        swapped = pltpu.roll(b, PATCH, 1)
        after = pltpu.roll(jnp.where(lane == half, swapped, b), BLOCK - 1, 1)
        before = pltpu.roll(jnp.where(lane == half - 1, swapped, b), 1, 1)
        pair = after + before
        twice = b + b
        soft_ref[t] = 0.25 * (twice + pair)
        step_ref[t] = after - before
        bend_ref[t] = twice - pair
        power_ref[pl.ds(t, 1), :] = jnp.sum(b * b, axis=0, keepdims=True)
        return carry

    lax.fori_loop(0, tall_ref.shape[0], filtered, 0, unroll=2)
    power_ref[...] = per_patch(power_ref[...])


def own_rim(offset_ref, rim_ref, out_ref):
    wide = rim_ref.shape[0]

    def one(k, carry):
        out_ref[k] = render_rows(rim_ref[k].astype(F32), None, offset_ref[0, wide + k], offset_ref[1, wide + k])
        return carry

    lax.fori_loop(0, wide, one, 0, unroll=2)


def render_rim(offsets, rim):
    return pl.pallas_call(
        own_rim,
        out_shape=shape(rim.shape, F32),
        in_specs=[spec(SMEM), spec(VMEM)],
        out_specs=spec(VMEM),
        compiler_params=params(),
        cost_estimate=pl.CostEstimate(flops=600_000, bytes_accessed=400_000, transcendentals=0),
    )(offsets, rim)


def own_strip(slot_ref, offset_ref, deep_ref, shallow_ref, rim_ref, image_ref, soft_ref, step_ref, bend_ref, power_ref, tall_ref, sums_ref):
    wide = rim_ref.shape[0]
    tiles = 2 * wide
    half = PATCH // 2
    for strip in range(2):

        def one(k, carried, strip=strip):
            b = strip * wide + k
            s = slot_ref[b]
            square = jnp.concatenate([shallow_ref[s], deep_ref[s]], 0).astype(F32)
            made = render_rows(square, None, offset_ref[0, b], offset_ref[1, b])
            image_ref[pl.ds(strip * BLOCK, BLOCK), pl.ds(pl.multiple_of(k * BLOCK, BLOCK), BLOCK)] = made
            tile = joined(made, carried)
            middle = tile[half : half + PATCH]
            tall_ref[b] = middle
            sums_ref[pl.ds(b, 1), :] = jnp.sum(middle, axis=0, keepdims=True)
            tall_ref[tiles + b, pl.ds(half, half), :] = tile[:half]
            low = jnp.sum(tile[:half], axis=0, keepdims=True)
            if strip == 0:
                tall_ref[tiles + wide + b, pl.ds(0, half), :] = tile[half + PATCH :]
                sums_ref[pl.ds(tiles + wide + b, 1), :] = jnp.sum(tile[half + PATCH :], axis=0, keepdims=True)
                sums_ref[pl.ds(tiles + b, 1), :] = low
            else:
                sums_ref[pl.ds(tiles + b, 1), :] += low
            return made

        lax.fori_loop(0, wide, one, jnp.zeros((BLOCK, BLOCK), F32))

    def rim_one(k, carried):
        made = rim_ref[k]
        tile = joined(made, carried)
        tall_ref[tiles + k, pl.ds(0, half), :] = tile
        sums_ref[pl.ds(tiles + k, 1), :] += jnp.sum(tile, axis=0, keepdims=True)
        return made

    lax.fori_loop(0, wide, rim_one, jnp.zeros((half, BLOCK), F32), unroll=2)
    filter_tiles(tall_ref, sums_ref, soft_ref, step_ref, bend_ref, power_ref)


def render_strip(slot, offsets, deep, shallow, rim, rows, cols):
    tiles = 2 * slot.shape[0]
    tile = shape((tiles, PATCH, BLOCK), F32)
    return pl.pallas_call(
        own_strip,
        out_shape=(shape((rows, cols), F32), tile, tile, tile, shape((tiles, BLOCK), F32)),
        in_specs=[spec(SMEM)] * 2 + [spec(VMEM)] * 3,
        out_specs=(spec(VMEM),) * 5,
        scratch_shapes=[VMEM((tiles, PATCH, BLOCK), F32), VMEM((tiles, BLOCK), F32)],
        compiler_params=params(),
        cost_estimate=pl.CostEstimate(flops=12_000_000, bytes_accessed=3_000_000, transcendentals=0),
    )(slot, offsets, deep, shallow, rim)


PAD = 8


def keep_tile(tile, t, tiles_ref, sums_ref):
    tiles_ref[t, pl.ds(PAD, PATCH), :] = tile
    tiles_ref[t, pl.ds(PAD - 1, 1), :] = tile[PATCH - 1 :]
    tiles_ref[t, pl.ds(PAD + PATCH, 1), :] = tile[:1]
    sums_ref[pl.ds(t, 1), :] = jnp.sum(tile, axis=0, keepdims=True)


def correlate(own_is_first, base, tiles_ref, sums_ref, acc_ref, soft_ref, step_ref, bend_ref, power_ref):
    area = float(PATCH * PATCH)
    tiles = sums_ref.shape[0]
    sums_ref[...] = per_patch(sums_ref[...]) / area

    def one(t, carry):
        mean = sums_ref[pl.ds(t, 1), :]
        o = tiles_ref[t, pl.ds(PAD, PATCH), :]
        after = tiles_ref[t, pl.ds(PAD + 1, PATCH), :]
        before = tiles_ref[t, pl.ds(PAD - 1, PATCH), :]
        pair = after + before
        twice = o + o
        soft = 0.25 * (twice + pair) - mean
        step = after - before
        bend = twice - pair
        flat = o - mean
        own_soft = soft_ref[base + t]
        products = (flat * flat, own_soft * step, own_soft * bend, step_ref[base + t] * soft, bend_ref[base + t] * soft)
        for q, product in enumerate(products):
            acc_ref[pl.ds(q * tiles + t, 1), :] = jnp.sum(product, axis=0, keepdims=True)
        return carry

    lax.fori_loop(0, tiles, one, 0, unroll=2)
    totals = per_patch(acc_ref[...])
    part = [totals[q * tiles : (q + 1) * tiles] for q in range(5)]
    scale = 1.0 / (jnp.sqrt(part[0] / area + tiny_value) * jnp.sqrt(power_ref[pl.ds(base, tiles), :] / area + tiny_value))
    signs = (1.0, -1.0) if own_is_first else (-1.0, 1.0)
    down = signs[0] * part[1] * scale / (2.0 * jnp.maximum(part[2] * scale, peak_floor))
    across = signs[1] * part[3] * scale / (2.0 * jnp.maximum(part[4] * scale, peak_floor))
    return down, across


def patch_row(values):
    lane = lax.broadcasted_iota(jnp.int32, values.shape, 1)
    row = lax.broadcasted_iota(jnp.int32, values.shape, 0)
    chosen = jnp.where(lane % 2 == 0, values, pltpu.roll(values, PATCH, 1))
    return jnp.sum(jnp.where(lane // 2 == row, chosen, 0.0), axis=0, keepdims=True)[:, : 2 * values.shape[0]]


def flow_scratch(tiles):
    return [
        VMEM((tiles, PATCH + 2 * PAD, BLOCK), F32),
        VMEM((tiles, BLOCK), F32),
        VMEM((5 * tiles, BLOCK), F32),
        VMEM((tiles, BLOCK), F32),
    ]


def flow_middle(offset_ref, other_ref, soft_ref, step_ref, bend_ref, power_ref, out_ref, tiles_ref, sums_ref, acc_ref, next_ref):
    tiles = sums_ref.shape[0]
    wide = tiles // 2
    next_ref[...] = other_ref[tiles, pl.ds(0, tiles), :].astype(F32)
    for strip in range(2):

        def one(k, carried, strip=strip):
            t = strip * wide + k
            made = render_rows(other_ref[t].astype(F32), next_ref[pl.ds(t, 1), :], offset_ref[0, t], offset_ref[1, t])
            keep_tile(joined(made, carried), t, tiles_ref, sums_ref)
            return made

        lax.fori_loop(0, wide, one, jnp.zeros((PATCH, BLOCK), F32), unroll=2)
    flows = correlate(False, 0, tiles_ref, sums_ref, acc_ref, soft_ref, step_ref, bend_ref, power_ref)
    for d, values in enumerate(flows):
        for strip in range(2):
            out_ref[d, pl.ds(strip, 1), :] = patch_row(values[strip * wide : (strip + 1) * wide])


def middle_flows(offsets, other, own):
    tiles = offsets.shape[1]
    return pl.pallas_call(
        flow_middle,
        out_shape=shape((2, 2, tiles), F32),
        in_specs=[spec(SMEM)] + [spec(VMEM)] * 5,
        out_specs=spec(VMEM),
        scratch_shapes=flow_scratch(tiles),
        compiler_params=params(),
        cost_estimate=pl.CostEstimate(flops=6_000_000, bytes_accessed=3_000_000, transcendentals=0),
    )(offsets, other, *own)


def flow_edges(
    offset_ref,
    rim_offset_ref,
    top_ref,
    shallow_ref,
    rim_ref,
    soft_ref,
    step_ref,
    bend_ref,
    power_ref,
    done_ref,
    out_ref,
    tiles_ref,
    sums_ref,
    acc_ref,
    next_ref,
):
    tiles = sums_ref.shape[0]
    wide = tiles // 2
    next_ref[...] = top_ref[wide].astype(F32)
    for strip in range(2):

        def one(k, carried, strip=strip):
            t = strip * wide + k
            if strip == 0:
                upper = render_rows(rim_ref[k].astype(F32), None, rim_offset_ref[0, wide + k], rim_offset_ref[1, wide + k])
            else:
                upper = render_rows(top_ref[k].astype(F32), None, offset_ref[0, k], offset_ref[1, k])
            lower = render_rows(shallow_ref[t].astype(F32), next_ref[pl.ds(t, 1), :], offset_ref[0, t], offset_ref[1, t])
            made = jnp.concatenate([upper, lower], 0)
            keep_tile(joined(made, carried), t, tiles_ref, sums_ref)
            return made

        lax.fori_loop(0, wide, one, jnp.zeros((PATCH, BLOCK), F32), unroll=2)
    flows = correlate(True, tiles, tiles_ref, sums_ref, acc_ref, soft_ref, step_ref, bend_ref, power_ref)
    for d, values in enumerate(flows):
        for strip in range(2):
            out_ref[d, pl.ds(2 * strip, 1), :] = patch_row(values[strip * wide : (strip + 1) * wide])
            out_ref[d, pl.ds(2 * strip + 1, 1), :] = done_ref[d, pl.ds(strip, 1), :]


def all_flows(offsets, rim_offsets, top, shallow, rim, own, done):
    tiles = offsets.shape[1]
    return pl.pallas_call(
        flow_edges,
        out_shape=shape((2, 4, tiles), F32),
        in_specs=[spec(SMEM)] * 2 + [spec(VMEM)] * 8,
        out_specs=spec(VMEM),
        scratch_shapes=flow_scratch(tiles),
        compiler_params=params(),
        cost_estimate=pl.CostEstimate(flops=6_000_000, bytes_accessed=3_000_000, transcendentals=0),
    )(offsets, rim_offsets, top, shallow, rim, *own, done)


def on_device(source, routes, offsets):
    strip = source[0]
    rows, cols = strip.shape
    route = routes[0]
    own_offsets = offsets[0]
    count = route.shape[0]
    devices = lax.axis_size("row")
    sections = lax.axis_size("sec")
    up = [(s, s - 1) for s in range(1, sections)]
    down = [(s, s + 1) for s in range(sections - 1)]
    below = [(r, r + 1) for r in range(devices - 1)]
    slanted = [
        (s * devices + r, (s - 1) * devices + r + 1) for s in range(1, sections) for r in range(devices - 1)
    ]

    owner = lax.div(route, jnp.int32(count))
    spot = lax.rem(route, jnp.int32(count))
    asked = owner[None, :] == jnp.arange(devices, dtype=jnp.int32)[:, None]
    lowest = jnp.min(jnp.where(asked, spot[None, :], count - 1), axis=1)
    highest = jnp.max(jnp.where(asked, spot[None, :], 0), axis=1)
    wanted = jnp.stack([lowest, highest], 1)[:, None, :]
    picked = lax.all_to_all(wanted, "row", 0, 0, tiled=True)
    blocks = blocks_of(strip)
    fellow = owner[:, None] == owner[None, :]
    lowest_here = jnp.min(jnp.where(fellow, spot[None, :], count), axis=1)
    slot = 2 * owner + (spot != lowest_here).astype(jnp.int32)

    other_offsets = lax.ppermute(own_offsets, "sec", up)
    former_offsets = lax.ppermute(own_offsets, "sec", down)
    rim_offsets = lax.ppermute(own_offsets, "row", below)
    other_rim_offsets = lax.ppermute(own_offsets, ("sec", "row"), slanted)

    out_deep = requested(picked, blocks, SPLIT, BLOCK - SPLIT)
    deep = lax.all_to_all(out_deep, "row", 0, 0, tiled=True)
    out_shallow = requested(picked, blocks, 0, SPLIT)
    shallow = lax.all_to_all(out_shallow, "row", 0, 0, tiled=True)

    middle, top_tail, bottom_tail = section_parts(slot, deep)
    former = lax.ppermute(middle, "sec", down)
    other_rim = lax.ppermute(bottom_tail, ("sec", "row"), slanted)
    other_top = lax.ppermute(top_tail, "sec", up)
    rim = lax.ppermute(bottom_tail, "row", below)
    own_shallow = shallow_part(slot, shallow)
    other_shallow = lax.ppermute(own_shallow, "sec", up)

    rim_made = render_rim(rim_offsets, rim)
    rendered, *own = render_strip(slot, own_offsets, deep, shallow, rim_made, rows, cols)
    middle_part = middle_flows(former_offsets, former, own)
    done = lax.ppermute(middle_part, "sec", up)
    flows = all_flows(other_offsets, other_rim_offsets, other_top, other_shallow, other_rim, own, done)
    return (rendered[None], flows[None])


def solution(mesh):
    placed = (P("sec", "row", None), P("sec", "row"), P("sec", None, "row"))

    return jax.shard_map(
        on_device,
        mesh=mesh,
        in_specs=placed,
        out_specs=(P("sec", "row", None), P("sec", None, "row", None)),
        check_vma=False,
    )
```

```python
import functools

import jax
import jax.numpy as jnp
from jax import lax
from jax.experimental import pallas as pl
from jax.experimental.pallas import tpu as pltpu
from jax.sharding import PartitionSpec as P


peak_floor = 64.0
tiny_value = 1e-06
BLOCK = 128
PATCH = 64
SPLIT = 32
VMEM = pltpu.VMEM
SMEM = pltpu.SMEM
F32 = jnp.float32
BF16 = jnp.bfloat16


def spec(space):
    return pl.BlockSpec(memory_space=space)


def shape(dims, dtype):
    return jax.ShapeDtypeStruct(dims, dtype)


def params(limit=14 << 20):
    return pltpu.CompilerParams(vmem_limit_bytes=limit)


def ask_blocks(route_ref, out_ref, slot_ref):
    devices = out_ref.shape[0]
    count = route_ref.shape[1]
    route = jnp.broadcast_to(route_ref[...], (devices, count))
    owner = lax.div(route, jnp.int32(count))
    spot = lax.rem(route, jnp.int32(count))
    asked = owner == lax.broadcasted_iota(jnp.int32, route.shape, 0)
    lowest = jnp.min(jnp.where(asked, spot, count - 1), axis=1, keepdims=True)
    highest = jnp.max(jnp.where(asked, spot, 0), axis=1, keepdims=True)
    lowest_here = jnp.sum(jnp.where(asked, lowest, 0), axis=0, keepdims=True)
    slot_ref[...] = 2 * owner[:1] + (spot[:1] != lowest_here).astype(jnp.int32)
    lane = lax.broadcasted_iota(jnp.int32, (devices, 2), 1)
    both = jnp.where(lane == 0, lowest, highest)
    for o in range(devices):
        out_ref[o] = both[o : o + 1]


def wanted_blocks(routes, devices):
    return pl.pallas_call(
        ask_blocks,
        out_shape=(shape((devices, 1, 2), jnp.int32), shape(routes.shape, jnp.int32)),
        in_specs=[spec(VMEM)],
        out_specs=(spec(VMEM), spec(VMEM)),
        compiler_params=params(),
    )(routes)


def cut_blocks(strip_ref, out_ref):
    wide = strip_ref.shape[1] // BLOCK
    for i in range(strip_ref.shape[0] // BLOCK):
        for k in range(wide):
            out_ref[i * wide + k] = strip_ref[i * BLOCK : (i + 1) * BLOCK, k * BLOCK : (k + 1) * BLOCK]


def blocks_of(strip):
    rows, cols = strip.shape
    return pl.pallas_call(
        cut_blocks,
        out_shape=shape((rows // BLOCK * (cols // BLOCK), BLOCK, BLOCK), strip.dtype),
        in_specs=[spec(VMEM)],
        out_specs=spec(VMEM),
        compiler_params=params(),
        cost_estimate=pl.CostEstimate(flops=0, bytes_accessed=2_000_000, transcendentals=0),
    )(strip)


def pack_requested(row_from, rows, picked_ref, blocks_ref, out_ref, sem):
    def one(i, carry):
        spot = picked_ref[i // 2, 0, i % 2]
        pltpu.make_async_copy(blocks_ref.at[spot, pl.ds(row_from, rows), :], out_ref.at[i], sem).start()
        return carry

    lax.fori_loop(0, out_ref.shape[0], one, 0, unroll=8)
    pltpu.make_async_copy(out_ref, out_ref, sem).wait()


def requested(picked, blocks, row_from, rows):
    slots = 2 * picked.shape[0]
    return pl.pallas_call(
        functools.partial(pack_requested, row_from, rows),
        out_shape=shape((slots, rows, BLOCK), blocks.dtype),
        in_specs=[spec(SMEM), spec(VMEM)],
        out_specs=spec(pl.ANY),
        scratch_shapes=[pltpu.SemaphoreType.DMA],
        compiler_params=params(55_000_000),
    )(picked, blocks)


def pack_middle(slot_ref, deep_ref, out_ref, next_ref):
    count = next_ref.shape[0]

    def one(b, carry):
        s = slot_ref[b]
        out_ref[b] = deep_ref[s, pl.ds(0, 64), :]
        next_ref[pl.ds(b, 1), :] = deep_ref[s, pl.ds(64, 16), :].astype(F32)[0:1]
        return carry

    lax.fori_loop(0, count, one, 0, unroll=8)
    out_ref[count, pl.ds(0, count), :] = next_ref[...].astype(BF16)
    out_ref[count, pl.ds(count, PATCH - count), :] = jnp.zeros((PATCH - count, BLOCK), BF16)


def middle_rows(slot, deep):
    count = slot.shape[0]
    return pl.pallas_call(
        pack_middle,
        out_shape=shape((count + 1, PATCH, BLOCK), BF16),
        in_specs=[spec(SMEM), spec(VMEM)],
        out_specs=spec(VMEM),
        scratch_shapes=[VMEM((count, BLOCK), F32)],
        compiler_params=params(),
    )(slot, deep)


def pack_tails(slot_ref, deep_ref, top_ref, bottom_ref, first_ref):
    half = bottom_ref.shape[0]

    def tails(b, carry):
        top = slot_ref[b]
        bottom = slot_ref[half + b]
        top_ref[b] = deep_ref[top, pl.ds(64, 32), :]
        bottom_ref[b] = deep_ref[bottom, pl.ds(64, 32), :]
        first_ref[pl.ds(b, 1), :] = deep_ref[top, pl.ds(0, 16), :].astype(F32)[0:1]
        first_ref[pl.ds(half + b, 1), :] = deep_ref[bottom, pl.ds(0, 16), :].astype(F32)[0:1]
        return carry

    lax.fori_loop(0, half, tails, 0, unroll=4)
    top_ref[half] = first_ref[...].astype(BF16)


def tail_rows(slot, deep):
    count = slot.shape[0]
    half = count // 2
    return pl.pallas_call(
        pack_tails,
        out_shape=(shape((half + 1, 32, BLOCK), BF16), shape((half, 32, BLOCK), BF16)),
        in_specs=[spec(SMEM), spec(VMEM)],
        out_specs=(spec(VMEM), spec(VMEM)),
        scratch_shapes=[VMEM((count, BLOCK), F32)],
        compiler_params=params(),
    )(slot, deep)


def pack_shallow(slot_ref, shallow_ref, out_ref):
    def one(b, carry):
        out_ref[b] = shallow_ref[slot_ref[b]]
        return carry

    lax.fori_loop(0, out_ref.shape[0], one, 0, unroll=4)


def shallow_part(slot, shallow):
    return pl.pallas_call(
        pack_shallow,
        out_shape=shape((slot.shape[0], *shallow.shape[1:]), BF16),
        in_specs=[spec(SMEM), spec(VMEM)],
        out_specs=spec(VMEM),
        compiler_params=params(),
    )(slot, shallow)


def mixed_across(square, across):
    lane = lax.broadcasted_iota(jnp.int32, square.shape, 1)
    moved = jnp.where(lane == BLOCK - 1, square, pltpu.roll(square, BLOCK - 1, 1))
    return (1.0 - across) * square + across * moved


def render_rows(square, following, downward, across):
    rows = square.shape[0]
    mixed = mixed_across(square, across)
    below = mixed if following is None else mixed_across(following, across)
    row = lax.broadcasted_iota(jnp.int32, square.shape, 0)
    moved = jnp.where(row == rows - 1, below, pltpu.roll(mixed, rows - 1, 0))
    return (1.0 - downward) * mixed + downward * moved


def joined(made, carried):
    lane = lax.broadcasted_iota(jnp.int32, made.shape, 1)
    return jnp.where(lane < BLOCK - PATCH // 2, made, carried)


def same_patch():
    half = PATCH // 2
    one = lax.broadcasted_iota(jnp.int32, (BLOCK, BLOCK), 0)
    two = lax.broadcasted_iota(jnp.int32, (BLOCK, BLOCK), 1)
    return ((((one + half) // PATCH) % 2) == (((two + half) // PATCH) % 2)).astype(F32)


def per_patch(values):
    return jnp.dot(values, same_patch(), precision=lax.Precision.HIGHEST)


def row_filters():
    half = PATCH // 2
    source = lax.broadcasted_iota(jnp.int32, (BLOCK, BLOCK), 0)
    target = lax.broadcasted_iota(jnp.int32, (BLOCK, BLOCK), 1)
    place = target % PATCH
    after = jnp.where(place == half - 1, target + 1 - PATCH, target + 1) % BLOCK
    before = jnp.where(place == half, target - 1 + PATCH, target - 1) % BLOCK
    after = (source == after).astype(F32)
    before = (source == before).astype(F32)
    itself = (source == target).astype(F32)
    pair = after + before
    twice = itself + itself
    return jnp.concatenate([0.25 * (twice + pair), after - before, twice - pair], 1).astype(BF16)


def folded(values):
    return jnp.sum(values.reshape(-1, 8, BLOCK), axis=0)


def write_filters(out_ref):
    filters = row_filters()
    out_ref[pl.ds(0, BLOCK), :] = filters
    out_ref[pl.ds(BLOCK, BLOCK), :] = filters


def filter_matrix():
    return pl.pallas_call(
        write_filters,
        out_shape=shape((2 * BLOCK, 3 * BLOCK), BF16),
        out_specs=spec(VMEM),
        compiler_params=params(),
    )()


def filter_tile(b, filter_ref, t, soft_ref, step_ref, bend_ref, parts_ref):
    high = b.astype(BF16)
    rest = (b - high.astype(F32)).astype(BF16)
    made = jnp.dot(jnp.concatenate([high, rest], 1), filter_ref[...], preferred_element_type=F32)
    soft_ref[t] = made[:, :BLOCK]
    step_ref[t] = made[:, BLOCK : 2 * BLOCK]
    bend_ref[t] = made[:, 2 * BLOCK :]
    parts_ref[t] = folded(b * b)


def own_strip(
    slot_ref, offset_ref, deep_ref, shallow_ref, filter_ref, image_ref, first_ref, soft_ref, step_ref, bend_ref, power_ref, mixed_ref, tall_ref, parts_ref, sums_ref, sem
):
    wide = first_ref.shape[0]
    half = PATCH // 2
    rows = 2 * BLOCK

    def across(b, carry):
        s = slot_ref[b]
        square = jnp.concatenate([shallow_ref[s], deep_ref[s]], 0)
        mixed = mixed_across(square.astype(F32), offset_ref[1, b])
        mixed_ref[b, pl.ds(0, BLOCK), :] = mixed
        mixed_ref[b, pl.ds(BLOCK, 1), :] = mixed[BLOCK - 1 :]
        return carry

    lax.fori_loop(0, 2 * wide, across, 0, unroll=8)
    tall_ref[0] = jnp.zeros((rows, BLOCK), F32)

    def down(k, carry):
        for strip in range(2):
            b = strip * wide + k
            y = offset_ref[0, b]
            made = (1.0 - y) * mixed_ref[b, pl.ds(0, BLOCK), :] + y * mixed_ref[b, pl.ds(1, BLOCK), :]
            tall_ref[k + 1, pl.ds(strip * BLOCK, BLOCK), :] = made
            if strip == 0:
                first_ref[k] = made[:half]
        pltpu.make_async_copy(
            tall_ref.at[k + 1], image_ref.at[:, pl.ds(pl.multiple_of(k * BLOCK, BLOCK), BLOCK)], sem
        ).start()
        return carry

    lax.fori_loop(0, wide, down, 0, unroll=4)
    groups = (1, 3, 2)

    def tile(k, g):
        rows_of = pl.ds(g * PATCH - half, PATCH)
        return joined(tall_ref[k + 1, rows_of, :], tall_ref[k, rows_of, :])

    def add_up(k, carry):
        for i, g in enumerate(groups):
            parts_ref[i * wide + k] = folded(tile(k, g))
        return carry

    lax.fori_loop(0, wide, add_up, 0, unroll=4)
    sums_ref[...] = per_patch(jnp.sum(parts_ref[...], axis=1)) / float(PATCH * PATCH)

    def filtered(k, carry):
        for i, g in enumerate(groups):
            t = i * wide + k
            filter_tile(tile(k, g) - sums_ref[pl.ds(t, 1), :], filter_ref, t, soft_ref, step_ref, bend_ref, parts_ref)
        return carry

    lax.fori_loop(0, wide, filtered, 0, unroll=4)
    power_ref[...] = per_patch(jnp.sum(parts_ref[...], axis=1))
    pltpu.make_async_copy(image_ref, image_ref, sem).wait()


def tile_outs(tiles):
    tile = shape((tiles, PATCH, BLOCK), F32)
    return (tile, tile, tile, shape((tiles, BLOCK), F32))


def render_strip(slot, offsets, deep, shallow, filters, rows, cols):
    blocks = slot.shape[0]
    wide = cols // BLOCK
    tiles = 3 * wide
    return pl.pallas_call(
        own_strip,
        out_shape=(shape((rows, cols), F32), shape((wide, PATCH // 2, BLOCK), F32), *tile_outs(tiles)),
        in_specs=[spec(SMEM)] * 2 + [spec(VMEM)] * 3,
        out_specs=(spec(pl.ANY),) + (spec(VMEM),) * 5,
        scratch_shapes=[
            VMEM((blocks, BLOCK + 8, BLOCK), F32),
            VMEM((wide + 1, rows, BLOCK), F32),
            VMEM((tiles, 8, BLOCK), F32),
            VMEM((tiles, BLOCK), F32),
            pltpu.SemaphoreType.DMA,
        ],
        compiler_params=params(),
        cost_estimate=pl.CostEstimate(flops=12_000_000, bytes_accessed=3_000_000, transcendentals=0),
    )(slot, offsets, deep, shallow, filters)


def own_zero(offset_ref, rim_ref, first_ref, filter_ref, soft_ref, step_ref, bend_ref, power_ref, tall_ref, parts_ref, sums_ref):
    wide = rim_ref.shape[0]

    def one(k, carried):
        made = render_rows(rim_ref[k].astype(F32), None, offset_ref[0, wide + k], offset_ref[1, wide + k])
        whole = jnp.concatenate([made, first_ref[k]], 0)
        tile = joined(whole, carried)
        tall_ref[k] = tile
        parts_ref[k] = folded(tile)
        return whole

    lax.fori_loop(0, wide, one, jnp.zeros((PATCH, BLOCK), F32), unroll=4)
    sums_ref[...] = per_patch(jnp.sum(parts_ref[...], axis=1)) / float(PATCH * PATCH)

    def filtered(k, carry):
        filter_tile(tall_ref[k] - sums_ref[pl.ds(k, 1), :], filter_ref, k, soft_ref, step_ref, bend_ref, parts_ref)
        return carry

    lax.fori_loop(0, wide, filtered, 0, unroll=8)
    power_ref[...] = per_patch(jnp.sum(parts_ref[...], axis=1))


def rim_tiles(offsets, rim, first, filters):
    wide = rim.shape[0]
    return pl.pallas_call(
        own_zero,
        out_shape=tile_outs(wide),
        in_specs=[spec(SMEM)] + [spec(VMEM)] * 3,
        out_specs=(spec(VMEM),) * 4,
        scratch_shapes=[VMEM((wide, PATCH, BLOCK), F32), VMEM((wide, 8, BLOCK), F32), VMEM((wide, BLOCK), F32)],
        compiler_params=params(),
        cost_estimate=pl.CostEstimate(flops=3_000_000, bytes_accessed=1_000_000, transcendentals=0),
    )(offsets, rim, first, filters)


PAD = 8


def keep_tile(tile, t, tiles_ref, sums_ref):
    tiles_ref[t, pl.ds(PAD, PATCH), :] = tile
    tiles_ref[t, pl.ds(PAD - 1, 1), :] = tile[PATCH - 1 :]
    tiles_ref[t, pl.ds(PAD + PATCH, 1), :] = tile[:1]
    sums_ref[pl.ds(t, 1), :] = jnp.sum(tile, axis=0, keepdims=True)


def correlate(own_is_first, own, tiles_ref, sums_ref, acc_ref):
    area = float(PATCH * PATCH)
    tiles = sums_ref.shape[0]
    wide = tiles // 2
    sums_ref[...] = per_patch(sums_ref[...]) / area
    for strip, (refs, base) in enumerate(own):
        soft_ref, step_ref, bend_ref, _ = refs

        def one(k, carry, strip=strip, base=base, soft_ref=soft_ref, step_ref=step_ref, bend_ref=bend_ref):
            t = strip * wide + k
            mean = sums_ref[pl.ds(t, 1), :]
            o = tiles_ref[t, pl.ds(PAD, PATCH), :]
            after = tiles_ref[t, pl.ds(PAD + 1, PATCH), :]
            before = tiles_ref[t, pl.ds(PAD - 1, PATCH), :]
            pair = after + before
            twice = o + o
            soft = 0.25 * (twice + pair) - mean
            step = after - before
            bend = twice - pair
            flat = o - mean
            own_soft = soft_ref[base + k]
            products = (flat * flat, own_soft * step, own_soft * bend, step_ref[base + k] * soft, bend_ref[base + k] * soft)
            for q, product in enumerate(products):
                acc_ref[pl.ds(q * tiles + t, 1), :] = jnp.sum(product, axis=0, keepdims=True)
            return carry

        lax.fori_loop(0, wide, one, 0, unroll=2)
    totals = per_patch(acc_ref[...])
    part = [totals[q * tiles : (q + 1) * tiles] for q in range(5)]
    power = jnp.concatenate([refs[3][pl.ds(base, wide), :] for refs, base in own], 0)
    scale = 1.0 / (jnp.sqrt(part[0] / area + tiny_value) * jnp.sqrt(power / area + tiny_value))
    signs = (1.0, -1.0) if own_is_first else (-1.0, 1.0)
    down = signs[0] * part[1] * scale / (2.0 * jnp.maximum(part[2] * scale, peak_floor))
    across = signs[1] * part[3] * scale / (2.0 * jnp.maximum(part[4] * scale, peak_floor))
    return down, across


def patch_row(values):
    lane = lax.broadcasted_iota(jnp.int32, values.shape, 1)
    row = lax.broadcasted_iota(jnp.int32, values.shape, 0)
    chosen = jnp.where(lane % 2 == 0, values, pltpu.roll(values, PATCH, 1))
    return jnp.sum(jnp.where(lane // 2 == row, chosen, 0.0), axis=0, keepdims=True)[:, : 2 * values.shape[0]]


def flow_scratch(tiles):
    return [
        VMEM((tiles, PATCH + 2 * PAD, BLOCK), F32),
        VMEM((tiles, BLOCK), F32),
        VMEM((5 * tiles, BLOCK), F32),
        VMEM((tiles, BLOCK), F32),
    ]


def flow_middle(offset_ref, other_ref, soft_ref, step_ref, bend_ref, power_ref, out_ref, tiles_ref, sums_ref, acc_ref, next_ref):
    tiles = sums_ref.shape[0]
    wide = tiles // 2
    next_ref[...] = other_ref[tiles, pl.ds(0, tiles), :].astype(F32)
    for strip in range(2):

        def one(k, carried, strip=strip):
            t = strip * wide + k
            made = render_rows(other_ref[t].astype(F32), next_ref[pl.ds(t, 1), :], offset_ref[0, t], offset_ref[1, t])
            keep_tile(joined(made, carried), t, tiles_ref, sums_ref)
            return made

        lax.fori_loop(0, wide, one, jnp.zeros((PATCH, BLOCK), F32), unroll=8)
    refs = (soft_ref, step_ref, bend_ref, power_ref)
    flows = correlate(False, ((refs, 0), (refs, wide)), tiles_ref, sums_ref, acc_ref)
    for d, values in enumerate(flows):
        for strip in range(2):
            out_ref[d, pl.ds(strip, 1), :] = patch_row(values[strip * wide : (strip + 1) * wide])


def middle_flows(offsets, other, own):
    tiles = offsets.shape[1]
    return pl.pallas_call(
        flow_middle,
        out_shape=shape((2, 2, tiles), F32),
        in_specs=[spec(SMEM)] + [spec(VMEM)] * 5,
        out_specs=spec(VMEM),
        scratch_shapes=flow_scratch(tiles),
        compiler_params=params(),
        cost_estimate=pl.CostEstimate(flops=6_000_000, bytes_accessed=3_000_000, transcendentals=0),
    )(offsets, other, *own)


def flow_edges(
    offset_ref,
    rim_offset_ref,
    top_ref,
    shallow_ref,
    rim_ref,
    *refs,
):
    zero_refs, own_refs, (out_ref, tiles_ref, sums_ref, acc_ref, next_ref) = refs[:4], refs[4:8], refs[8:]
    tiles = sums_ref.shape[0]
    wide = tiles // 2
    next_ref[...] = top_ref[wide].astype(F32)
    for strip in range(2):

        def one(k, carried, strip=strip):
            t = strip * wide + k
            if strip == 0:
                upper = render_rows(rim_ref[k].astype(F32), None, rim_offset_ref[0, wide + k], rim_offset_ref[1, wide + k])
            else:
                upper = render_rows(top_ref[k].astype(F32), None, offset_ref[0, k], offset_ref[1, k])
            lower = render_rows(shallow_ref[t].astype(F32), next_ref[pl.ds(t, 1), :], offset_ref[0, t], offset_ref[1, t])
            made = jnp.concatenate([upper, lower], 0)
            keep_tile(joined(made, carried), t, tiles_ref, sums_ref)
            return made

        lax.fori_loop(0, wide, one, jnp.zeros((PATCH, BLOCK), F32), unroll=8)
    flows = correlate(True, ((zero_refs, 0), (own_refs, tiles)), tiles_ref, sums_ref, acc_ref)
    for d, values in enumerate(flows):
        for strip in range(2):
            out_ref[d, pl.ds(strip, 1), :] = patch_row(values[strip * wide : (strip + 1) * wide])


def edge_flows(offsets, rim_offsets, top, shallow, rim, zero, own):
    tiles = offsets.shape[1]
    return pl.pallas_call(
        flow_edges,
        out_shape=shape((2, 2, tiles), F32),
        in_specs=[spec(SMEM)] * 2 + [spec(VMEM)] * 11,
        out_specs=spec(VMEM),
        scratch_shapes=flow_scratch(tiles),
        compiler_params=params(),
        cost_estimate=pl.CostEstimate(flops=6_000_000, bytes_accessed=3_000_000, transcendentals=0),
    )(offsets, rim_offsets, top, shallow, rim, *zero, *own)


def merge_rows(edge_ref, middle_ref, out_ref):
    for d in range(2):
        for i in range(2):
            out_ref[d, pl.ds(2 * i, 1), :] = edge_ref[d, pl.ds(i, 1), :]
            out_ref[d, pl.ds(2 * i + 1, 1), :] = middle_ref[d, pl.ds(i, 1), :]


def merge_flows(edge, middle):
    return pl.pallas_call(
        merge_rows,
        out_shape=shape((2, 4, edge.shape[2]), F32),
        in_specs=[spec(VMEM)] * 2,
        out_specs=spec(VMEM),
        compiler_params=params(),
    )(edge, middle)


def on_device(source, routes, offsets):
    strip = source[0]
    rows, cols = strip.shape
    own_offsets = offsets[0]
    count = routes.shape[1]
    devices = lax.axis_size("row")
    sections = lax.axis_size("sec")
    up = [(s, s - 1) for s in range(1, sections)]
    down = [(s, s + 1) for s in range(sections - 1)]
    below = [(r, r + 1) for r in range(devices - 1)]
    slanted = [
        (s * devices + r, (s - 1) * devices + r + 1) for s in range(1, sections) for r in range(devices - 1)
    ]

    wanted, slot = wanted_blocks(routes, devices)
    slot = slot.reshape(count)
    picked = lax.all_to_all(wanted, "row", 0, 0, tiled=True)
    blocks = blocks_of(strip)

    other_offsets = lax.ppermute(own_offsets, "sec", up)
    former_offsets = lax.ppermute(own_offsets, "sec", down)
    rim_offsets = lax.ppermute(own_offsets, "row", below)
    other_rim_offsets = lax.ppermute(own_offsets, ("sec", "row"), slanted)

    out_deep = requested(picked, blocks, SPLIT, BLOCK - SPLIT)
    deep = lax.all_to_all(out_deep, "row", 0, 0, tiled=True)
    out_shallow = requested(picked, blocks, 0, SPLIT)
    shallow = lax.all_to_all(out_shallow, "row", 0, 0, tiled=True)

    middle = middle_rows(slot, deep)
    former = lax.ppermute(middle, "sec", down)
    top_tail, bottom_tail = tail_rows(slot, deep)
    rim = lax.ppermute(bottom_tail, "row", below)
    other_rim = lax.ppermute(bottom_tail, ("sec", "row"), slanted)
    other_top = lax.ppermute(top_tail, "sec", up)
    filters = filter_matrix()
    own_shallow = shallow_part(slot, shallow)
    other_shallow = lax.ppermute(own_shallow, "sec", up)

    rendered, first, *own = render_strip(slot, own_offsets, deep, shallow, filters, rows, cols)
    zero = rim_tiles(rim_offsets, rim, first, filters)
    middle_part = middle_flows(former_offsets, former, own)
    done = lax.ppermute(middle_part, "sec", up)
    edge_part = edge_flows(other_offsets, other_rim_offsets, other_top, other_shallow, other_rim, zero, own)
    flows = merge_flows(edge_part, done)
    return (rendered[None], flows[None])


def solution(mesh):
    placed = (P("sec", "row", None), P("sec", "row"), P("sec", None, "row"))

    return jax.shard_map(
        on_device,
        mesh=mesh,
        in_specs=placed,
        out_specs=(P("sec", "row", None), P("sec", None, "row", None)),
        check_vma=False,
    )
```

```python
import functools

import jax
import jax.numpy as jnp
from jax import lax
from jax.experimental import pallas as pl
from jax.experimental.pallas import tpu as pltpu
from jax.sharding import PartitionSpec as P


peak_floor = 64.0
tiny_value = 1e-06
BLOCK = 128
PATCH = 64
SPLIT = 32
VMEM = pltpu.VMEM
SMEM = pltpu.SMEM
F32 = jnp.float32
BF16 = jnp.bfloat16


def spec(space):
    return pl.BlockSpec(memory_space=space)


def shape(dims, dtype):
    return jax.ShapeDtypeStruct(dims, dtype)


def params(limit=14 << 20):
    return pltpu.CompilerParams(vmem_limit_bytes=limit)


def ask_blocks(route_ref, out_ref, slot_ref):
    devices = out_ref.shape[0]
    count = route_ref.shape[1]
    route = jnp.broadcast_to(route_ref[...], (devices, count))
    owner = lax.div(route, jnp.int32(count))
    spot = lax.rem(route, jnp.int32(count))
    asked = owner == lax.broadcasted_iota(jnp.int32, route.shape, 0)
    lowest = jnp.min(jnp.where(asked, spot, count - 1), axis=1, keepdims=True)
    highest = jnp.max(jnp.where(asked, spot, 0), axis=1, keepdims=True)
    lowest_here = jnp.sum(jnp.where(asked, lowest, 0), axis=0, keepdims=True)
    slot_ref[...] = 2 * owner[:1] + (spot[:1] != lowest_here).astype(jnp.int32)
    lane = lax.broadcasted_iota(jnp.int32, (devices, 2), 1)
    both = jnp.where(lane == 0, lowest, highest)
    for o in range(devices):
        out_ref[o] = both[o : o + 1]


def wanted_blocks(routes, devices):
    return pl.pallas_call(
        ask_blocks,
        out_shape=(shape((devices, 1, 2), jnp.int32), shape(routes.shape, jnp.int32)),
        in_specs=[spec(VMEM)],
        out_specs=(spec(VMEM), spec(VMEM)),
        compiler_params=params(),
    )(routes)


def cut_blocks(strip_ref, out_ref):
    wide = strip_ref.shape[1] // BLOCK
    for i in range(strip_ref.shape[0] // BLOCK):
        for k in range(wide):
            out_ref[i * wide + k] = strip_ref[i * BLOCK : (i + 1) * BLOCK, k * BLOCK : (k + 1) * BLOCK]


def blocks_of(strip):
    rows, cols = strip.shape
    return pl.pallas_call(
        cut_blocks,
        out_shape=shape((rows // BLOCK * (cols // BLOCK), BLOCK, BLOCK), strip.dtype),
        in_specs=[spec(VMEM)],
        out_specs=spec(VMEM),
        compiler_params=params(),
        cost_estimate=pl.CostEstimate(flops=0, bytes_accessed=2_000_000, transcendentals=0),
    )(strip)


def pack_requested(row_from, rows, picked_ref, blocks_ref, out_ref, sem):
    def one(i, carry):
        spot = picked_ref[i // 2, 0, i % 2]
        pltpu.make_async_copy(blocks_ref.at[spot, pl.ds(row_from, rows), :], out_ref.at[i], sem).start()
        return carry

    lax.fori_loop(0, out_ref.shape[0], one, 0, unroll=64)
    pltpu.make_async_copy(out_ref, out_ref, sem).wait()


def requested(picked, blocks, row_from, rows):
    slots = 2 * picked.shape[0]
    return pl.pallas_call(
        functools.partial(pack_requested, row_from, rows),
        out_shape=shape((slots, rows, BLOCK), blocks.dtype),
        in_specs=[spec(SMEM), spec(VMEM)],
        out_specs=spec(pl.ANY),
        scratch_shapes=[pltpu.SemaphoreType.DMA],
        compiler_params=params(55_000_000),
    )(picked, blocks)


def pack_middle(slot_ref, deep_ref, out_ref, next_ref):
    count = next_ref.shape[0]

    def one(b, carry):
        s = slot_ref[b]
        out_ref[b] = deep_ref[s, pl.ds(0, 64), :]
        next_ref[pl.ds(b, 1), :] = deep_ref[s, pl.ds(64, 16), :].astype(F32)[0:1]
        return carry

    lax.fori_loop(0, count, one, 0, unroll=8)
    out_ref[count, pl.ds(0, count), :] = next_ref[...].astype(BF16)
    out_ref[count, pl.ds(count, PATCH - count), :] = jnp.zeros((PATCH - count, BLOCK), BF16)


def middle_rows(slot, deep):
    count = slot.shape[0]
    return pl.pallas_call(
        pack_middle,
        out_shape=shape((count + 1, PATCH, BLOCK), BF16),
        in_specs=[spec(SMEM), spec(VMEM)],
        out_specs=spec(VMEM),
        scratch_shapes=[VMEM((count, BLOCK), F32)],
        compiler_params=params(),
    )(slot, deep)


def pack_tails(slot_ref, deep_ref, top_ref, bottom_ref, first_ref):
    half = bottom_ref.shape[0]

    def tails(b, carry):
        top = slot_ref[b]
        bottom = slot_ref[half + b]
        top_ref[b] = deep_ref[top, pl.ds(64, 32), :]
        bottom_ref[b] = deep_ref[bottom, pl.ds(64, 32), :]
        first_ref[pl.ds(b, 1), :] = deep_ref[top, pl.ds(0, 16), :].astype(F32)[0:1]
        first_ref[pl.ds(half + b, 1), :] = deep_ref[bottom, pl.ds(0, 16), :].astype(F32)[0:1]
        return carry

    lax.fori_loop(0, half, tails, 0, unroll=4)
    top_ref[half] = first_ref[...].astype(BF16)


def tail_rows(slot, deep):
    count = slot.shape[0]
    half = count // 2
    return pl.pallas_call(
        pack_tails,
        out_shape=(shape((half + 1, 32, BLOCK), BF16), shape((half, 32, BLOCK), BF16)),
        in_specs=[spec(SMEM), spec(VMEM)],
        out_specs=(spec(VMEM), spec(VMEM)),
        scratch_shapes=[VMEM((count, BLOCK), F32)],
        compiler_params=params(),
    )(slot, deep)


def pack_shallow(slot_ref, shallow_ref, out_ref):
    def one(b, carry):
        out_ref[b] = shallow_ref[slot_ref[b]]
        return carry

    lax.fori_loop(0, out_ref.shape[0], one, 0, unroll=4)


def shallow_part(slot, shallow):
    return pl.pallas_call(
        pack_shallow,
        out_shape=shape((slot.shape[0], *shallow.shape[1:]), BF16),
        in_specs=[spec(SMEM), spec(VMEM)],
        out_specs=spec(VMEM),
        compiler_params=params(),
    )(slot, shallow)


def mixed_across(square, across):
    lane = lax.broadcasted_iota(jnp.int32, square.shape, 1)
    moved = jnp.where(lane == BLOCK - 1, square, pltpu.roll(square, BLOCK - 1, 1))
    return (1.0 - across) * square + across * moved


def render_rows(square, following, downward, across):
    rows = square.shape[0]
    mixed = mixed_across(square, across)
    below = mixed if following is None else mixed_across(following, across)
    row = lax.broadcasted_iota(jnp.int32, square.shape, 0)
    moved = jnp.where(row == rows - 1, below, pltpu.roll(mixed, rows - 1, 0))
    return (1.0 - downward) * mixed + downward * moved


def joined(made, carried):
    lane = lax.broadcasted_iota(jnp.int32, made.shape, 1)
    return jnp.where(lane < BLOCK - PATCH // 2, made, carried)


def same_patch():
    half = PATCH // 2
    one = lax.broadcasted_iota(jnp.int32, (BLOCK, BLOCK), 0)
    two = lax.broadcasted_iota(jnp.int32, (BLOCK, BLOCK), 1)
    return ((((one + half) // PATCH) % 2) == (((two + half) // PATCH) % 2)).astype(F32)


def per_patch(values):
    return jnp.dot(values, same_patch(), precision=lax.Precision.HIGHEST)


def row_filters():
    half = PATCH // 2
    source = lax.broadcasted_iota(jnp.int32, (BLOCK, BLOCK), 0)
    target = lax.broadcasted_iota(jnp.int32, (BLOCK, BLOCK), 1)
    place = target % PATCH
    after = jnp.where(place == half - 1, target + 1 - PATCH, target + 1) % BLOCK
    before = jnp.where(place == half, target - 1 + PATCH, target - 1) % BLOCK
    after = (source == after).astype(F32)
    before = (source == before).astype(F32)
    itself = (source == target).astype(F32)
    pair = after + before
    twice = itself + itself
    return jnp.concatenate([0.25 * (twice + pair), after - before, twice - pair], 1).astype(BF16)


def folded(values):
    return jnp.sum(values.reshape(-1, 8, BLOCK), axis=0)


def write_filters(out_ref):
    filters = row_filters()
    out_ref[pl.ds(0, BLOCK), :] = filters
    out_ref[pl.ds(BLOCK, BLOCK), :] = filters


def filter_matrix():
    return pl.pallas_call(
        write_filters,
        out_shape=shape((2 * BLOCK, 3 * BLOCK), BF16),
        out_specs=spec(VMEM),
        compiler_params=params(),
    )()


def filter_tile(b, filter_ref, t, soft_ref, step_ref, bend_ref, parts_ref):
    high = b.astype(BF16)
    rest = (b - high.astype(F32)).astype(BF16)
    made = jnp.dot(jnp.concatenate([high, rest], 1), filter_ref[...], preferred_element_type=F32)
    soft_ref[t] = made[:, :BLOCK]
    step_ref[t] = made[:, BLOCK : 2 * BLOCK]
    bend_ref[t] = made[:, 2 * BLOCK :]
    parts_ref[t] = folded(b * b)


def own_strip(
    slot_ref, offset_ref, deep_ref, shallow_ref, filter_ref, image_ref, first_ref, soft_ref, step_ref, bend_ref, power_ref, mixed_ref, tall_ref, parts_ref, sums_ref, sem
):
    wide = first_ref.shape[0]
    half = PATCH // 2
    rows = 2 * BLOCK

    def across(b, carry):
        s = slot_ref[b]
        square = jnp.concatenate([shallow_ref[s], deep_ref[s]], 0)
        mixed = mixed_across(square.astype(F32), offset_ref[1, b])
        mixed_ref[b, pl.ds(0, BLOCK), :] = mixed
        mixed_ref[b, pl.ds(BLOCK, 1), :] = mixed[BLOCK - 1 :]
        return carry

    lax.fori_loop(0, 2 * wide, across, 0, unroll=8)
    tall_ref[0] = jnp.zeros((rows, BLOCK), F32)

    def down(k, carry):
        for strip in range(2):
            b = strip * wide + k
            y = offset_ref[0, b]
            made = (1.0 - y) * mixed_ref[b, pl.ds(0, BLOCK), :] + y * mixed_ref[b, pl.ds(1, BLOCK), :]
            tall_ref[k + 1, pl.ds(strip * BLOCK, BLOCK), :] = made
            if strip == 0:
                first_ref[k] = made[:half]
        pltpu.make_async_copy(
            tall_ref.at[k + 1], image_ref.at[:, pl.ds(pl.multiple_of(k * BLOCK, BLOCK), BLOCK)], sem
        ).start()
        return carry

    lax.fori_loop(0, wide, down, 0, unroll=4)
    groups = (1, 3, 2)

    def tile(k, g):
        rows_of = pl.ds(g * PATCH - half, PATCH)
        return joined(tall_ref[k + 1, rows_of, :], tall_ref[k, rows_of, :])

    def add_up(k, carry):
        for i, g in enumerate(groups):
            parts_ref[i * wide + k] = folded(tile(k, g))
        return carry

    lax.fori_loop(0, wide, add_up, 0, unroll=4)
    sums_ref[...] = per_patch(jnp.sum(parts_ref[...], axis=1)) / float(PATCH * PATCH)

    def filtered(k, carry):
        for i, g in enumerate(groups):
            t = i * wide + k
            filter_tile(tile(k, g) - sums_ref[pl.ds(t, 1), :], filter_ref, t, soft_ref, step_ref, bend_ref, parts_ref)
        return carry

    lax.fori_loop(0, wide, filtered, 0, unroll=4)
    power_ref[...] = per_patch(jnp.sum(parts_ref[...], axis=1))
    pltpu.make_async_copy(image_ref, image_ref, sem).wait()


def tile_outs(tiles):
    tile = shape((tiles, PATCH, BLOCK), F32)
    return (tile, tile, tile, shape((tiles, BLOCK), F32))


def render_strip(slot, offsets, deep, shallow, filters, rows, cols):
    blocks = slot.shape[0]
    wide = cols // BLOCK
    tiles = 3 * wide
    return pl.pallas_call(
        own_strip,
        out_shape=(shape((rows, cols), F32), shape((wide, PATCH // 2, BLOCK), F32), *tile_outs(tiles)),
        in_specs=[spec(SMEM)] * 2 + [spec(VMEM)] * 3,
        out_specs=(spec(pl.ANY),) + (spec(VMEM),) * 5,
        scratch_shapes=[
            VMEM((blocks, BLOCK + 8, BLOCK), F32),
            VMEM((wide + 1, rows, BLOCK), F32),
            VMEM((tiles, 8, BLOCK), F32),
            VMEM((tiles, BLOCK), F32),
            pltpu.SemaphoreType.DMA,
        ],
        compiler_params=params(),
        cost_estimate=pl.CostEstimate(flops=12_000_000, bytes_accessed=3_000_000, transcendentals=0),
    )(slot, offsets, deep, shallow, filters)


def own_zero(offset_ref, rim_ref, first_ref, filter_ref, soft_ref, step_ref, bend_ref, power_ref, tall_ref, parts_ref, sums_ref):
    wide = rim_ref.shape[0]

    def one(k, carried):
        made = render_rows(rim_ref[k].astype(F32), None, offset_ref[0, wide + k], offset_ref[1, wide + k])
        whole = jnp.concatenate([made, first_ref[k]], 0)
        tile = joined(whole, carried)
        tall_ref[k] = tile
        parts_ref[k] = folded(tile)
        return whole

    lax.fori_loop(0, wide, one, jnp.zeros((PATCH, BLOCK), F32), unroll=4)
    sums_ref[...] = per_patch(jnp.sum(parts_ref[...], axis=1)) / float(PATCH * PATCH)

    def filtered(k, carry):
        filter_tile(tall_ref[k] - sums_ref[pl.ds(k, 1), :], filter_ref, k, soft_ref, step_ref, bend_ref, parts_ref)
        return carry

    lax.fori_loop(0, wide, filtered, 0, unroll=8)
    power_ref[...] = per_patch(jnp.sum(parts_ref[...], axis=1))


def rim_tiles(offsets, rim, first, filters):
    wide = rim.shape[0]
    return pl.pallas_call(
        own_zero,
        out_shape=tile_outs(wide),
        in_specs=[spec(SMEM)] + [spec(VMEM)] * 3,
        out_specs=(spec(VMEM),) * 4,
        scratch_shapes=[VMEM((wide, PATCH, BLOCK), F32), VMEM((wide, 8, BLOCK), F32), VMEM((wide, BLOCK), F32)],
        compiler_params=params(),
        cost_estimate=pl.CostEstimate(flops=3_000_000, bytes_accessed=1_000_000, transcendentals=0),
    )(offsets, rim, first, filters)


PAD = 8


def keep_tile(tile, t, tiles_ref, sums_ref):
    tiles_ref[t, pl.ds(PAD, PATCH), :] = tile
    tiles_ref[t, pl.ds(PAD - 1, 1), :] = tile[PATCH - 1 :]
    tiles_ref[t, pl.ds(PAD + PATCH, 1), :] = tile[:1]
    sums_ref[pl.ds(t, 1), :] = jnp.sum(tile, axis=0, keepdims=True)


def correlate(own_is_first, own, tiles_ref, sums_ref, acc_ref):
    area = float(PATCH * PATCH)
    tiles = sums_ref.shape[0]
    wide = tiles // 2
    sums_ref[...] = per_patch(sums_ref[...]) / area
    for strip, (refs, base) in enumerate(own):
        soft_ref, step_ref, bend_ref, _ = refs

        def one(k, carry, strip=strip, base=base, soft_ref=soft_ref, step_ref=step_ref, bend_ref=bend_ref):
            t = strip * wide + k
            mean = sums_ref[pl.ds(t, 1), :]
            o = tiles_ref[t, pl.ds(PAD, PATCH), :]
            after = tiles_ref[t, pl.ds(PAD + 1, PATCH), :]
            before = tiles_ref[t, pl.ds(PAD - 1, PATCH), :]
            pair = after + before
            twice = o + o
            soft = 0.25 * (twice + pair) - mean
            step = after - before
            bend = twice - pair
            flat = o - mean
            own_soft = soft_ref[base + k]
            products = (flat * flat, own_soft * step, own_soft * bend, step_ref[base + k] * soft, bend_ref[base + k] * soft)
            for q, product in enumerate(products):
                acc_ref[pl.ds(q * tiles + t, 1), :] = jnp.sum(product, axis=0, keepdims=True)
            return carry

        lax.fori_loop(0, wide, one, 0, unroll=4)
    totals = per_patch(acc_ref[...])
    part = [totals[q * tiles : (q + 1) * tiles] for q in range(5)]
    power = jnp.concatenate([refs[3][pl.ds(base, wide), :] for refs, base in own], 0)
    scale = 1.0 / (jnp.sqrt(part[0] / area + tiny_value) * jnp.sqrt(power / area + tiny_value))
    signs = (1.0, -1.0) if own_is_first else (-1.0, 1.0)
    down = signs[0] * part[1] * scale / (2.0 * jnp.maximum(part[2] * scale, peak_floor))
    across = signs[1] * part[3] * scale / (2.0 * jnp.maximum(part[4] * scale, peak_floor))
    return down, across


def patch_row(values):
    lane = lax.broadcasted_iota(jnp.int32, values.shape, 1)
    row = lax.broadcasted_iota(jnp.int32, values.shape, 0)
    chosen = jnp.where(lane % 2 == 0, values, pltpu.roll(values, PATCH, 1))
    return jnp.sum(jnp.where(lane // 2 == row, chosen, 0.0), axis=0, keepdims=True)[:, : 2 * values.shape[0]]


def flow_scratch(tiles):
    return [
        VMEM((tiles, PATCH + 2 * PAD, BLOCK), F32),
        VMEM((tiles, BLOCK), F32),
        VMEM((5 * tiles, BLOCK), F32),
        VMEM((tiles, BLOCK), F32),
    ]


def flow_middle(offset_ref, other_ref, soft_ref, step_ref, bend_ref, power_ref, out_ref, tiles_ref, sums_ref, acc_ref, next_ref):
    tiles = sums_ref.shape[0]
    wide = tiles // 2
    next_ref[...] = other_ref[tiles, pl.ds(0, tiles), :].astype(F32)
    for strip in range(2):

        def one(k, carried, strip=strip):
            t = strip * wide + k
            made = render_rows(other_ref[t].astype(F32), next_ref[pl.ds(t, 1), :], offset_ref[0, t], offset_ref[1, t])
            keep_tile(joined(made, carried), t, tiles_ref, sums_ref)
            return made

        lax.fori_loop(0, wide, one, jnp.zeros((PATCH, BLOCK), F32), unroll=16)
    refs = (soft_ref, step_ref, bend_ref, power_ref)
    flows = correlate(False, ((refs, 0), (refs, wide)), tiles_ref, sums_ref, acc_ref)
    for d, values in enumerate(flows):
        for strip in range(2):
            out_ref[d, pl.ds(strip, 1), :] = patch_row(values[strip * wide : (strip + 1) * wide])


def middle_flows(offsets, other, own):
    tiles = offsets.shape[1]
    return pl.pallas_call(
        flow_middle,
        out_shape=shape((2, 2, tiles), F32),
        in_specs=[spec(SMEM)] + [spec(VMEM)] * 5,
        out_specs=spec(VMEM),
        scratch_shapes=flow_scratch(tiles),
        compiler_params=params(),
        cost_estimate=pl.CostEstimate(flops=6_000_000, bytes_accessed=3_000_000, transcendentals=0),
    )(offsets, other, *own)


def flow_edges(
    offset_ref,
    rim_offset_ref,
    top_ref,
    shallow_ref,
    rim_ref,
    *refs,
):
    zero_refs, own_refs, (out_ref, tiles_ref, sums_ref, acc_ref, next_ref) = refs[:4], refs[4:8], refs[8:]
    tiles = sums_ref.shape[0]
    wide = tiles // 2
    next_ref[...] = top_ref[wide].astype(F32)
    for strip in range(2):

        def one(k, carried, strip=strip):
            t = strip * wide + k
            if strip == 0:
                upper = render_rows(rim_ref[k].astype(F32), None, rim_offset_ref[0, wide + k], rim_offset_ref[1, wide + k])
            else:
                upper = render_rows(top_ref[k].astype(F32), None, offset_ref[0, k], offset_ref[1, k])
            lower = render_rows(shallow_ref[t].astype(F32), next_ref[pl.ds(t, 1), :], offset_ref[0, t], offset_ref[1, t])
            made = jnp.concatenate([upper, lower], 0)
            keep_tile(joined(made, carried), t, tiles_ref, sums_ref)
            return made

        lax.fori_loop(0, wide, one, jnp.zeros((PATCH, BLOCK), F32), unroll=16)
    flows = correlate(True, ((zero_refs, 0), (own_refs, tiles)), tiles_ref, sums_ref, acc_ref)
    for d, values in enumerate(flows):
        for strip in range(2):
            out_ref[d, pl.ds(strip, 1), :] = patch_row(values[strip * wide : (strip + 1) * wide])


def edge_flows(offsets, rim_offsets, top, shallow, rim, zero, own):
    tiles = offsets.shape[1]
    return pl.pallas_call(
        flow_edges,
        out_shape=shape((2, 2, tiles), F32),
        in_specs=[spec(SMEM)] * 2 + [spec(VMEM)] * 11,
        out_specs=spec(VMEM),
        scratch_shapes=flow_scratch(tiles),
        compiler_params=params(),
        cost_estimate=pl.CostEstimate(flops=6_000_000, bytes_accessed=3_000_000, transcendentals=0),
    )(offsets, rim_offsets, top, shallow, rim, *zero, *own)


def merge_rows(edge_ref, middle_ref, out_ref):
    for d in range(2):
        for i in range(2):
            out_ref[d, pl.ds(2 * i, 1), :] = edge_ref[d, pl.ds(i, 1), :]
            out_ref[d, pl.ds(2 * i + 1, 1), :] = middle_ref[d, pl.ds(i, 1), :]


def merge_flows(edge, middle):
    return pl.pallas_call(
        merge_rows,
        out_shape=shape((2, 4, edge.shape[2]), F32),
        in_specs=[spec(VMEM)] * 2,
        out_specs=spec(VMEM),
        compiler_params=params(),
    )(edge, middle)


def on_device(source, routes, offsets):
    strip = source[0]
    rows, cols = strip.shape
    own_offsets = offsets[0]
    count = routes.shape[1]
    devices = lax.axis_size("row")
    sections = lax.axis_size("sec")
    up = [(s, s - 1) for s in range(1, sections)]
    down = [(s, s + 1) for s in range(sections - 1)]
    below = [(r, r + 1) for r in range(devices - 1)]
    slanted = [
        (s * devices + r, (s - 1) * devices + r + 1) for s in range(1, sections) for r in range(devices - 1)
    ]

    wanted, slot = wanted_blocks(routes, devices)
    slot = slot.reshape(count)
    picked = lax.all_to_all(wanted, "row", 0, 0, tiled=True)
    blocks = blocks_of(strip)

    other_offsets = lax.ppermute(own_offsets, "sec", up)
    former_offsets = lax.ppermute(own_offsets, "sec", down)
    rim_offsets = lax.ppermute(own_offsets, "row", below)
    other_rim_offsets = lax.ppermute(own_offsets, ("sec", "row"), slanted)

    out_deep = requested(picked, blocks, SPLIT, BLOCK - SPLIT)
    deep = lax.all_to_all(out_deep, "row", 0, 0, tiled=True)
    out_shallow = requested(picked, blocks, 0, SPLIT)
    shallow = lax.all_to_all(out_shallow, "row", 0, 0, tiled=True)

    middle = middle_rows(slot, deep)
    former = lax.ppermute(middle, "sec", down)
    top_tail, bottom_tail = tail_rows(slot, deep)
    rim = lax.ppermute(bottom_tail, "row", below)
    other_rim = lax.ppermute(bottom_tail, ("sec", "row"), slanted)
    other_top = lax.ppermute(top_tail, "sec", up)
    filters = filter_matrix()
    own_shallow = shallow_part(slot, shallow)
    other_shallow = lax.ppermute(own_shallow, "sec", up)

    rendered, first, *own = render_strip(slot, own_offsets, deep, shallow, filters, rows, cols)
    zero = rim_tiles(rim_offsets, rim, first, filters)
    middle_part = middle_flows(former_offsets, former, own)
    done = lax.ppermute(middle_part, "sec", up)
    edge_part = edge_flows(other_offsets, other_rim_offsets, other_top, other_shallow, other_rim, zero, own)
    flows = merge_flows(edge_part, done)
    return (rendered[None], flows[None])


def solution(mesh):
    placed = (P("sec", "row", None), P("sec", "row"), P("sec", None, "row"))

    return jax.shard_map(
        on_device,
        mesh=mesh,
        in_specs=placed,
        out_specs=(P("sec", "row", None), P("sec", None, "row", None)),
        check_vma=False,
    )
```
